32 devices in a mesh: rep: 4 (over x, core), shard: 8 (over z, y).
Axes of the slice: x: 2, y: 2, z: 4, core: 2. Of those that a mesh axis runs over, the one named last changes fastest.
Arguments:
- tokens: bfloat16 [4096, 896], P(('rep', 'shard')), may hold values from -6 to 6
- cotangent: bfloat16 [4096, 896], P(('rep', 'shard')), may hold values from -6 to 6
- lengths: int32 [32, 8], P(('rep', 'shard')), may hold values from 1 to 64, 128 in all within a row
- query_weight: bfloat16 [896, 896], P('shard'), may hold values from -0.1875 to 0.1875
- key_weight: bfloat16 [896, 128], P('shard'), may hold values from -0.1875 to 0.1875
- value_weight: bfloat16 [896, 128], P('shard'), may hold values from -0.1875 to 0.1875
- output_weight: bfloat16 [896, 896], P('shard'), may hold values from -0.5 to 0.5
- query_bias: bfloat16 [896], P('shard'), may hold values from -3 to 3
- key_bias: bfloat16 [128], P('shard'), may hold values from -3 to 3
- value_bias: bfloat16 [128], P('shard'), may hold values from -3 to 3
- attn_gain: bfloat16 [896], P('shard'), may hold values from 0.5 to 1.5
- gate_weight: bfloat16 [896, 4864], P('shard'), may hold values from -0.1875 to 0.1875
- up_weight: bfloat16 [896, 4864], P('shard'), may hold values from -0.1875 to 0.1875
- down_weight: bfloat16 [4864, 896], P('shard'), may hold values from -0.15625 to 0.15625
- mlp_gain: bfloat16 [896], P('shard'), may hold values from 0.5 to 1.5
Outputs:
- result: bfloat16 [4096, 896], P(('rep', 'shard'))
- grad_tokens: float32 [4096, 896], P(('rep', 'shard'))
- grad_query_weight: float32 [896, 896], P('shard')
- grad_key_weight: float32 [896, 128], P('shard')
- grad_value_weight: float32 [896, 128], P('shard')
- grad_output_weight: float32 [896, 896], P('shard')
- grad_query_bias: float32 [896], P('shard')
- grad_key_bias: float32 [128], P('shard')
- grad_value_bias: float32 [128], P('shard')
- grad_attn_gain: float32 [896], P('shard')
- grad_gate_weight: float32 [896, 4864], P('shard')
- grad_up_weight: float32 [896, 4864], P('shard')
- grad_down_weight: float32 [4864, 896], P('shard')
- grad_mlp_gain: float32 [896], P('shard')
The draws below stay inside these ranges and needn't reach their ends.
Inputs may be any that keep to these rules, and one draw needn't show every extreme that they name: Row b lists the lengths of the 8 sequences packed in order on the b-th block of 128 tokens; they fill it exactly, and the longest of every row is exactly 64.
All inputs are finite; a program needn't handle non-finite values.
Results may differ from the reference program's by a relative error of at most 0.02.
The reference program's roundings to bfloat16 on the way count: a program that leaves them out, or rounds other values in their place, can miss the bound.
Values may be sent and summed in bfloat16 or wider, within the bound.
A program may use at most 192 MiB of HBM per device.

```python
import math
import jax
import jax.numpy as jnp
import numpy as np
from jax import lax

D = 896
HEADS = 14
KVH = 2
HD = 64
FF = 4864
TOK_DEV = 128
SEQS = 8
KVD = 128
MAXLEN = 64
DEVBLK = 32
TOKENS = 4096


def block_levels(key, extent, pieces, least, largest):
    def one(position, parts):
        draws = jax.random.uniform(jax.random.fold_in(jax.random.fold_in(key, 6), position), (parts,), jnp.float32, least / len(pieces), largest / len(pieces))
        return jnp.repeat(jnp.exp(draws), extent[position] // parts).reshape((-1,) + (1,) * (len(extent) - position - 1))

    factor_of = one(*pieces[0])
    for cut in pieces[1:]:
        factor_of = factor_of * one(*cut)
    return factor_of


def length_profile(number_of, total, most, lean):
    weights = [(1 << 20) // math.isqrt(standing ** lean) + 1 for standing in range(2, number_of + 1)]
    rest, holding = total - most - (number_of - 1), [1] * (number_of - 1)
    while rest > 0:
        movable = [i for i in range(number_of - 1) if holding[i] < most]
        pool, left = sum([weights[i] for i in movable]), rest
        for i in movable:
            more = min(most - holding[i], max(1, left * weights[i] // pool), rest)
            holding[i] = holding[i] + more
            rest = rest - more
    return np.array([most] + holding)


def ragged_sizes(rng, number_of, total, bound, lean):
    if number_of == 2:
        one = jax.random.randint(rng, (), max(1, total - bound), min(bound, total - 1) + 1)
        return jnp.stack([one, total - one])
    tallies = jnp.asarray(length_profile(number_of, total, bound, lean), jnp.int32)
    twos = (number_of - 1) // 2
    source_of, receiver = tallies[1:1 + 2 * twos:2], tallies[2:2 + 2 * twos:2]
    room = jnp.minimum(source_of - 1, bound - receiver)
    shifted = jax.random.randint(jax.random.fold_in(rng, 1), (twos,), 0, 1 << 20) % (room + 1)
    tallies = tallies.at[1:1 + 2 * twos:2].set(source_of - shifted).at[2:2 + 2 * twos:2].set(receiver + shifted)
    return tallies[jax.random.permutation(jax.random.fold_in(rng, 2), number_of)]


def noise(key, dims, scale, most, pieces=(), kind=jnp.bfloat16):
    entries = scale * jax.random.normal(key, dims, jnp.float32)
    if pieces:
        entries = entries * block_levels(key, dims, pieces, -0.22, 0.18)
    return jnp.clip(entries, -most, most).astype(kind)


def setup_inputs(seed: int = 0) -> dict:
    splits = jax.random.split(jax.random.key(seed), 16)
    tokens = noise(splits[0], (TOKENS, D), 1.0, 6.0, ((0, 32),))
    cotangent = noise(splits[1], (TOKENS, D), 1.0, 6.0, ((0, 32),))
    lengths = jax.vmap(lambda own: ragged_sizes(own, SEQS, TOK_DEV, MAXLEN, 2))(jax.random.split(splits[2], DEVBLK)).reshape((DEVBLK, SEQS)).astype(jnp.int32)
    query_weight = noise(splits[3], (D, D), D ** -0.5, 0.1875, ((0, 8),))
    key_weight = noise(splits[4], (D, KVD), D ** -0.5, 0.1875, ((0, 8),))
    value_weight = noise(splits[5], (D, KVD), D ** -0.5, 0.1875, ((0, 8),))
    output_weight = noise(splits[6], (D, D), (D // 8) ** -0.5, 0.5, ((0, 8),))
    query_bias = noise(splits[7], (D,), 0.5, 3.0, ((0, 8),))
    key_bias = noise(splits[8], (KVD,), 0.5, 3.0, ((0, 8),))
    value_bias = noise(splits[9], (KVD,), 0.5, 3.0, ((0, 8),))
    attn_gain = jnp.clip(1.0 + 0.1 * jax.random.normal(splits[10], (D,), jnp.float32), 0.5, 1.5).astype(jnp.bfloat16)
    gate_weight = noise(splits[11], (D, FF), D ** -0.5, 0.1875, ((0, 8),))
    up_weight = noise(splits[12], (D, FF), D ** -0.5, 0.1875, ((0, 8),))
    down_weight = noise(splits[13], (FF, D), (FF // 4) ** -0.5, 0.15625, ((0, 8),))
    mlp_gain = jnp.clip(1.0 + 0.1 * jax.random.normal(splits[14], (D,), jnp.float32), 0.5, 1.5).astype(jnp.bfloat16)
    return dict(tokens=tokens, cotangent=cotangent, lengths=lengths, query_weight=query_weight, key_weight=key_weight, value_weight=value_weight, output_weight=output_weight, query_bias=query_bias, key_bias=key_bias, value_bias=value_bias, attn_gain=attn_gain, gate_weight=gate_weight, up_weight=up_weight, down_weight=down_weight, mlp_gain=mlp_gain)


theta_base = 1000000.0
eps_norm = 1e-06
masked_score = -1000000000.0

def tables(lengths_row, rows):
    ends = jnp.cumsum(lengths_row)
    starts = ends - lengths_row
    places = jnp.arange(rows, dtype=jnp.int32)
    inside = ((places[:, None] >= starts[None, :]) & (places[:, None] < ends[None, :])).astype(jnp.int32)
    slots = jnp.arange(lengths_row.shape[0], dtype=jnp.int32)
    segment = lax.optimization_barrier(jnp.sum(inside * slots[None, :], axis=1))
    first = lax.optimization_barrier(jnp.sum(inside * starts[None, :], axis=1))
    offset = (places - first).astype(jnp.float32)
    half = HD // 2
    freq = theta_base ** (-(jnp.arange(half, dtype=jnp.float32) * (2.0 / HD)))
    angles = offset[:, None] * freq[None, :]
    return (segment, places, jnp.cos(angles), jnp.sin(angles))

def rotate(values, cosine, sine):
    half = values.shape[-1] // 2
    first, second = (values[..., :half], values[..., half:])
    cosine = cosine[:, :, None, :]
    sine = sine[:, :, None, :]
    return jnp.concatenate([first * cosine - second * sine, second * cosine + first * sine], axis=-1)

def unrotate(grads, cosine, sine):
    half = grads.shape[-1] // 2
    first, second = (grads[..., :half], grads[..., half:])
    cosine = cosine[:, :, None, :]
    sine = sine[:, :, None, :]
    return jnp.concatenate([first * cosine + second * sine, second * cosine - first * sine], axis=-1)

def norm_fwd(hidden, gain):
    scale = lax.rsqrt(lax.optimization_barrier(jnp.mean(hidden * hidden, axis=-1, keepdims=True)) + eps_norm)
    return (scale, hidden * scale * gain.astype(jnp.float32))

def norm_bwd(dnormed, hidden, scale, gain):
    gain_f = gain.astype(jnp.float32)
    dgain = lax.optimization_barrier(jnp.sum(dnormed * hidden * scale, axis=0))
    inner = dnormed * gain_f
    dhidden = scale * inner - hidden * (scale * scale * scale) * lax.optimization_barrier(jnp.mean(inner * hidden, axis=-1, keepdims=True))
    return (dhidden, dgain)

def scores_of(query, keys, segment, places):
    raw = jnp.einsum('igha,jga->ghij', query.astype(jnp.float32), keys.astype(jnp.float32)) * (1.0 / math.sqrt(HD))
    allowed = (segment[:, None] == segment[None, :]) & (places[None, :] <= places[:, None])
    return jnp.where(allowed[None, None], raw, masked_score)

def attend(query, keys, values, segment, places):
    raw = scores_of(query, keys, segment, places)
    top = lax.optimization_barrier(jnp.max(raw, axis=-1, keepdims=True))
    total = lax.optimization_barrier(jnp.sum(jnp.exp(raw - top), axis=-1))
    lse = top[..., 0] + jnp.log(total)
    probs = jnp.exp(raw - lse[..., None]).astype(jnp.bfloat16)
    mixed = jnp.einsum('ghij,jga->igha', probs.astype(jnp.float32), values.astype(jnp.float32)).astype(jnp.bfloat16)
    return (mixed, lse)

def attend_back(query, keys, values, mixed, dmixed, lse, segment, places):
    raw = scores_of(query, keys, segment, places)
    probs_f = jnp.exp(raw - lse[..., None])
    probs = probs_f.astype(jnp.bfloat16)
    dvals = jnp.einsum('ghij,igha->jga', probs.astype(jnp.float32), dmixed.astype(jnp.float32))
    dprobs = jnp.einsum('igha,jga->ghij', dmixed.astype(jnp.float32), values.astype(jnp.float32))
    delta = jnp.einsum('igha,igha->ghi', dmixed.astype(jnp.float32), mixed.astype(jnp.float32))
    dscores = (probs_f * (dprobs - delta[..., None]) * (1.0 / math.sqrt(HD))).astype(jnp.bfloat16)
    dquery = jnp.einsum('ghij,jga->igha', dscores.astype(jnp.float32), keys.astype(jnp.float32))
    dkeys = jnp.einsum('ghij,igha->jga', dscores.astype(jnp.float32), query.astype(jnp.float32))
    return (dquery, dkeys, dvals)

def forward(tokens, lengths, attn_params, mlp_params):
    blocks, rows, width = tokens.shape
    query_weight, key_weight, value_weight, output_weight, query_bias, key_bias, value_bias, attn_gain = attn_params
    gate_weight, up_weight, down_weight, mlp_gain = mlp_params
    segment, places, cosine, sine = jax.vmap(lambda lens: tables(lens, rows))(lengths)
    flat = tokens.reshape(blocks * rows, width).astype(jnp.float32)
    scale_one, normed_one = norm_fwd(flat, attn_gain)
    normed_one = normed_one.astype(jnp.bfloat16)
    query = jnp.dot(normed_one, query_weight, preferred_element_type=jnp.float32) + query_bias.astype(jnp.float32)
    keys = jnp.dot(normed_one, key_weight, preferred_element_type=jnp.float32) + key_bias.astype(jnp.float32)
    values = jnp.dot(normed_one, value_weight, preferred_element_type=jnp.float32) + value_bias.astype(jnp.float32)
    query = rotate(query.reshape(blocks, rows, HEADS, HD), cosine, sine).astype(jnp.bfloat16)
    query = query.reshape(blocks, rows, KVH, HEADS // KVH, HD)
    keys = rotate(keys.reshape(blocks, rows, KVH, HD), cosine, sine).astype(jnp.bfloat16)
    values = values.reshape(blocks, rows, KVH, HD).astype(jnp.bfloat16)
    mixed, lse = jax.vmap(attend)(query, keys, values, segment, places)
    mixed_flat = mixed.reshape(blocks * rows, width)
    hidden_one = flat + jnp.dot(mixed_flat, output_weight, preferred_element_type=jnp.float32)
    scale_two, normed_two = norm_fwd(hidden_one, mlp_gain)
    normed_two = normed_two.astype(jnp.bfloat16)
    gate = jnp.dot(normed_two, gate_weight, preferred_element_type=jnp.float32)
    upper = jnp.dot(normed_two, up_weight, preferred_element_type=jnp.float32)
    product = (jax.nn.silu(gate) * upper).astype(jnp.bfloat16)
    result = (hidden_one + jnp.dot(product, down_weight, preferred_element_type=jnp.float32)).astype(jnp.bfloat16)
    saved = (segment, places, cosine, sine, flat, scale_one, normed_one, query, keys, values, mixed, lse, hidden_one, scale_two, normed_two, gate, upper, product)
    return (result.reshape(blocks, rows, width), saved)

def backward(cotangent, saved, attn_params, mlp_params):
    blocks, rows, width = cotangent.shape
    query_weight, key_weight, value_weight, output_weight, query_bias, key_bias, value_bias, attn_gain = attn_params
    gate_weight, up_weight, down_weight, mlp_gain = mlp_params
    segment, places, cosine, sine, flat, scale_one, normed_one, query, keys, values, mixed, lse, hidden_one, scale_two, normed_two, gate, upper, product = saved
    cot_b = cotangent.reshape(blocks * rows, width)
    cot_f = cot_b.astype(jnp.float32)
    grad_down = jnp.dot(product.T, cot_b, preferred_element_type=jnp.float32)
    dprod = jnp.dot(cot_b, down_weight.T, preferred_element_type=jnp.float32)
    sigma = jax.nn.sigmoid(gate)
    dgate = (dprod * upper * sigma * (1.0 + gate * (1.0 - sigma))).astype(jnp.bfloat16)
    dup = (dprod * gate * sigma).astype(jnp.bfloat16)
    grad_gate = jnp.dot(normed_two.T, dgate, preferred_element_type=jnp.float32)
    grad_up = jnp.dot(normed_two.T, dup, preferred_element_type=jnp.float32)
    dnormed_two = jnp.dot(dgate, gate_weight.T, preferred_element_type=jnp.float32) + jnp.dot(dup, up_weight.T, preferred_element_type=jnp.float32)
    dh_two, grad_mlp_gain = norm_bwd(dnormed_two, hidden_one, scale_two, mlp_gain)
    dhidden = cot_f + dh_two
    dres = dhidden.astype(jnp.bfloat16)
    mixed_flat = mixed.reshape(blocks * rows, width)
    grad_output = jnp.dot(mixed_flat.T, dres, preferred_element_type=jnp.float32)
    dmixed = jnp.dot(dres, output_weight.T, preferred_element_type=jnp.float32).astype(jnp.bfloat16)
    dmixed = dmixed.reshape(blocks, rows, KVH, HEADS // KVH, HD)
    dquery, dkeys, dvals = jax.vmap(attend_back)(query, keys, values, mixed, dmixed, lse, segment, places)
    dquery = unrotate(dquery.reshape(blocks, rows, HEADS, HD), cosine, sine).reshape(blocks * rows, width)
    dkeys = unrotate(dkeys, cosine, sine).reshape(blocks * rows, KVH * HD)
    dvals = dvals.reshape(blocks * rows, KVH * HD)
    grad_qbias = lax.optimization_barrier(jnp.sum(dquery, axis=0))
    grad_kbias = lax.optimization_barrier(jnp.sum(dkeys, axis=0))
    grad_vbias = lax.optimization_barrier(jnp.sum(dvals, axis=0))
    dquery_b = dquery.astype(jnp.bfloat16)
    dkeys_b = dkeys.astype(jnp.bfloat16)
    dvals_b = dvals.astype(jnp.bfloat16)
    grad_query = jnp.dot(normed_one.T, dquery_b, preferred_element_type=jnp.float32)
    grad_key = jnp.dot(normed_one.T, dkeys_b, preferred_element_type=jnp.float32)
    grad_value = jnp.dot(normed_one.T, dvals_b, preferred_element_type=jnp.float32)
    dnormed_one = jnp.dot(dquery_b, query_weight.T, preferred_element_type=jnp.float32) + jnp.dot(dkeys_b, key_weight.T, preferred_element_type=jnp.float32) + jnp.dot(dvals_b, value_weight.T, preferred_element_type=jnp.float32)
    dh_one, grad_attn_gain = norm_bwd(dnormed_one, flat, scale_one, attn_gain)
    grad_input = (dhidden + dh_one).reshape(blocks, rows, width)
    attn_grads = (grad_query, grad_key, grad_value, grad_output, grad_qbias, grad_kbias, grad_vbias, grad_attn_gain)
    mlp_grads = (grad_gate, grad_up, grad_down, grad_mlp_gain)
    return (grad_input, attn_grads, mlp_grads)

def reference(tokens, cotangent, lengths, query_weight, key_weight, value_weight, output_weight, query_bias, key_bias, value_bias, attn_gain, gate_weight, up_weight, down_weight, mlp_gain):
    attn_params = (query_weight, key_weight, value_weight, output_weight, query_bias, key_bias, value_bias, attn_gain)
    mlp_params = (gate_weight, up_weight, down_weight, mlp_gain)
    count = lengths.shape[0]
    group = math.gcd(count, max(1, 4096 // TOK_DEV))
    rounds = count // group
    tok_groups = tokens.reshape(rounds, group, TOK_DEV, D)
    cot_groups = cotangent.reshape(rounds, group, TOK_DEV, D)
    len_groups = lengths.reshape(rounds, group, SEQS)
    zeros = jax.tree.map(lambda weight: jnp.zeros(weight.shape, jnp.float32), (attn_params, mlp_params))

    def advance(carry, items):
        tok_block, cot_block, len_block = items
        result, saved = forward(tok_block, len_block, attn_params, mlp_params)
        grad_input, attn_grads, mlp_grads = backward(cot_block, saved, attn_params, mlp_params)
        carry = jax.tree.map(lambda left, right: left + right, carry, (attn_grads, mlp_grads))
        return (carry, (result, grad_input))
    totals, outputs = lax.scan(advance, zeros, (tok_groups, cot_groups, len_groups))
    attn_total, mlp_total = totals
    results = outputs[0].reshape(TOKENS, D)
    grads_in = outputs[1].reshape(TOKENS, D)
    return (results, grads_in, attn_total[0], attn_total[1], attn_total[2], attn_total[3], attn_total[4], attn_total[5], attn_total[6], attn_total[7], mlp_total[0], mlp_total[1], mlp_total[2], mlp_total[3])
```

```python
import math

import jax
import jax.numpy as jnp
from jax import lax
from jax.sharding import PartitionSpec as P

HEADS = 14
KVH = 2
HD = 64


theta_base = 1000000.0
eps_norm = 1e-06
masked_score = -1000000000.0


def times_transposed(left, weight):
    return lax.dot_general(
        left, weight, (((1,), (1,)), ((), ())), preferred_element_type=jnp.float32
    )


def tables(lengths_row, rows):
    ends = jnp.cumsum(lengths_row)
    starts = ends - lengths_row
    places = jnp.arange(rows, dtype=jnp.int32)
    inside = ((places[:, None] >= starts[None, :]) & (places[:, None] < ends[None, :])).astype(
        jnp.int32
    )
    slots = jnp.arange(lengths_row.shape[0], dtype=jnp.int32)
    segment = jnp.sum(inside * slots[None, :], axis=1)
    first = jnp.sum(inside * starts[None, :], axis=1)
    offset = (places - first).astype(jnp.float32)
    half = HD // 2
    freq = theta_base ** (-(jnp.arange(half, dtype=jnp.float32) * (2.0 / HD)))
    angles = offset[:, None] * freq[None, :]
    return (segment, places, jnp.cos(angles), jnp.sin(angles))


def rotate(values, cosine, sine):
    half = values.shape[-1] // 2
    first, second = (values[..., :half], values[..., half:])
    cosine = cosine[:, :, None, :]
    sine = sine[:, :, None, :]
    return jnp.concatenate(
        [first * cosine - second * sine, second * cosine + first * sine], axis=-1
    )


def unrotate(grads, cosine, sine):
    half = grads.shape[-1] // 2
    first, second = (grads[..., :half], grads[..., half:])
    cosine = cosine[:, :, None, :]
    sine = sine[:, :, None, :]
    return jnp.concatenate(
        [first * cosine + second * sine, second * cosine - first * sine], axis=-1
    )


def norm_fwd(hidden, gain):
    scale = lax.rsqrt(jnp.mean(hidden * hidden, axis=-1, keepdims=True) + eps_norm)
    return (scale, hidden * scale * gain.astype(jnp.float32))


def norm_bwd(dnormed, hidden, scale, gain):
    gain_f = gain.astype(jnp.float32)
    dgain = jnp.sum(dnormed * hidden * scale, axis=0)
    inner = dnormed * gain_f
    dhidden = scale * inner - hidden * (scale * scale * scale) * jnp.mean(
        inner * hidden, axis=-1, keepdims=True
    )
    return (dhidden, dgain)


def scores_of(query, keys, segment, places):
    raw = jnp.einsum("igha,jga->ghij", query, keys, preferred_element_type=jnp.float32) * (
        1.0 / math.sqrt(HD)
    )
    allowed = (segment[:, None] == segment[None, :]) & (places[None, :] <= places[:, None])
    return jnp.where(allowed[None, None], raw, masked_score)


def attend(query, keys, values, segment, places):
    raw = scores_of(query, keys, segment, places)
    top = jnp.max(raw, axis=-1, keepdims=True)
    total = jnp.sum(jnp.exp(raw - top), axis=-1)
    lse = top[..., 0] + jnp.log(total)
    probs = jnp.exp(raw - lse[..., None]).astype(jnp.bfloat16)
    mixed = jnp.einsum("ghij,jga->igha", probs, values, preferred_element_type=jnp.float32).astype(
        jnp.bfloat16
    )
    return (mixed, lse)


def attend_back(query, keys, values, mixed, dmixed, lse, segment, places):
    raw = scores_of(query, keys, segment, places)
    probs_f = jnp.exp(raw - lse[..., None])
    probs = probs_f.astype(jnp.bfloat16)
    dvals = jnp.einsum("ghij,igha->jga", probs, dmixed, preferred_element_type=jnp.float32)
    dprobs = jnp.einsum("igha,jga->ghij", dmixed, values, preferred_element_type=jnp.float32)
    delta = jnp.einsum("igha,igha->ghi", dmixed, mixed, preferred_element_type=jnp.float32)
    dscores = (probs_f * (dprobs - delta[..., None]) * (1.0 / math.sqrt(HD))).astype(jnp.bfloat16)
    dquery = jnp.einsum("ghij,jga->igha", dscores, keys, preferred_element_type=jnp.float32)
    dkeys = jnp.einsum("ghij,igha->jga", dscores, query, preferred_element_type=jnp.float32)
    return (dquery, dkeys, dvals)


def pad_rows(vector, rows):
    return jnp.pad(vector, (0, rows - vector.shape[0]))


def share_of(weight, index, shards, shares):
    width = weight.shape[1] // shards
    part = width // shares
    return jnp.concatenate(
        [
            lax.dynamic_slice(weight, (0, s * width + index * part), (weight.shape[0], part))
            for s in range(shards)
        ],
        axis=1,
    )


def on_device(
    tokens,
    cotangent,
    lengths,
    query_weight,
    key_weight,
    value_weight,
    output_weight,
    query_bias,
    key_bias,
    value_bias,
    attn_gain,
    gate_weight,
    up_weight,
    down_weight,
    mlp_gain,
):
    shards = lax.axis_size("shard")
    reps = lax.axis_size("rep")
    rep = lax.axis_index("rep")
    rows, width = tokens.shape
    own = query_weight.shape[0]
    kvd = key_weight.shape[1]
    own_kv = key_bias.shape[0]
    small_w = 128
    f32, bf16 = jnp.float32, jnp.bfloat16

    small = jnp.stack(
        [query_bias, attn_gain, mlp_gain, pad_rows(key_bias, own), pad_rows(value_bias, own)],
        axis=1,
    )
    small = jnp.pad(small, ((0, 0), (0, small_w - small.shape[1])))
    packed = jnp.concatenate(
        [query_weight, key_weight, value_weight, output_weight, small], axis=1
    )
    packed = lax.all_gather(packed, "shard", axis=0, tiled=True)
    wide = width + 2 * kvd
    qkv_weight = packed[:, :wide]
    output_full = packed[:, wide : wide + width]
    vectors = packed[:, wide + width : wide + width + 5].T
    query_bias_f, attn_gain_f, mlp_gain_f = vectors[0], vectors[1], vectors[2]
    key_bias_f = vectors[3].reshape(shards, own)[:, :own_kv].reshape(kvd)
    value_bias_f = vectors[4].reshape(shards, own)[:, :own_kv].reshape(kvd)
    qkv_bias = jnp.concatenate([query_bias_f, key_bias_f, value_bias_f]).astype(f32)

    part = down_weight.shape[0] // reps
    gate_mine = lax.all_gather(
        share_of(gate_weight, rep, shards, reps), "shard", axis=0, tiled=True
    )
    up_mine = lax.all_gather(share_of(up_weight, rep, shards, reps), "shard", axis=0, tiled=True)
    down_mine = lax.all_gather(
        lax.dynamic_slice(down_weight, (rep * part, 0), (part, width)),
        "shard",
        axis=0,
        tiled=True,
    )
    cot_all = lax.all_gather(cotangent, "rep", axis=0, tiled=True)

    segment, places, cosine, sine = jax.vmap(lambda lens: tables(lens, rows))(lengths)
    flat = tokens.astype(f32)
    scale_one, normed_one = norm_fwd(flat, attn_gain_f)
    normed_one = normed_one.astype(bf16)
    qkv = jnp.dot(normed_one, qkv_weight, preferred_element_type=f32) + qkv_bias
    query = rotate(qkv[:, :width].reshape(1, rows, HEADS, HD), cosine, sine).astype(bf16)
    query = query.reshape(1, rows, KVH, HEADS // KVH, HD)
    keys = rotate(qkv[:, width : width + kvd].reshape(1, rows, KVH, HD), cosine, sine).astype(bf16)
    values = qkv[:, width + kvd :].reshape(1, rows, KVH, HD).astype(bf16)
    mixed, lse = jax.vmap(attend)(query, keys, values, segment, places)
    mixed_flat = mixed.reshape(rows, width)
    hidden_one = flat + jnp.dot(mixed_flat, output_full, preferred_element_type=f32)
    scale_two, normed_two = norm_fwd(hidden_one, mlp_gain_f)
    normed_all = lax.all_gather(normed_two.astype(bf16), "rep", axis=0, tiled=True)

    gate = jnp.dot(normed_all, gate_mine, preferred_element_type=f32)
    upper = jnp.dot(normed_all, up_mine, preferred_element_type=f32)
    sigma = jax.nn.sigmoid(gate)
    product = (gate * sigma * upper).astype(bf16)
    dprod = times_transposed(cot_all, down_mine)
    dgate = (dprod * upper * sigma * (1.0 + gate * (1.0 - sigma))).astype(bf16)
    dup = (dprod * gate * sigma).astype(bf16)
    dnormed_part = times_transposed(dgate, gate_mine) + times_transposed(dup, up_mine)
    dnormed_two = lax.psum_scatter(
        dnormed_part.astype(bf16), "rep", scatter_dimension=0, tiled=True
    ).astype(f32)
    grad_down = jnp.dot(product.T, cot_all, preferred_element_type=f32).astype(bf16)
    grad_gate = jnp.dot(normed_all.T, dgate, preferred_element_type=f32).astype(bf16)
    grad_up = jnp.dot(normed_all.T, dup, preferred_element_type=f32).astype(bf16)
    down_owned = lax.psum_scatter(grad_down, "shard", scatter_dimension=0, tiled=True)
    gate_owned = lax.psum_scatter(grad_gate, "shard", scatter_dimension=0, tiled=True)
    up_owned = lax.psum_scatter(grad_up, "shard", scatter_dimension=0, tiled=True)
    out_part = jnp.dot(product, down_mine, preferred_element_type=f32).astype(bf16)
    out_sum = lax.psum_scatter(out_part, "rep", scatter_dimension=0, tiled=True)
    result = (hidden_one + out_sum.astype(f32)).astype(bf16)

    dh_two, grad_mlp_gain = norm_bwd(dnormed_two, hidden_one, scale_two, mlp_gain_f)
    dhidden = cotangent.astype(f32) + dh_two
    dres = dhidden.astype(bf16)
    grad_output = jnp.dot(mixed_flat.T, dres, preferred_element_type=f32).astype(bf16)
    dmixed = times_transposed(dres, output_full).astype(bf16)
    dmixed = dmixed.reshape(1, rows, KVH, HEADS // KVH, HD)
    dquery, dkeys, dvals = jax.vmap(attend_back)(
        query, keys, values, mixed, dmixed, lse, segment, places
    )
    dquery = unrotate(dquery.reshape(1, rows, HEADS, HD), cosine, sine).reshape(rows, width)
    dkeys = unrotate(dkeys, cosine, sine).reshape(rows, kvd)
    dvals = dvals.reshape(rows, kvd)
    dqkv = jnp.concatenate([dquery, dkeys, dvals], axis=1)
    grad_bias = jnp.sum(dqkv, axis=0)
    dqkv_b = dqkv.astype(bf16)
    grad_qkv = jnp.dot(normed_one.T, dqkv_b, preferred_element_type=f32).astype(bf16)
    dnormed_one = times_transposed(dqkv_b, qkv_weight)
    dh_one, grad_attn_gain = norm_bwd(dnormed_one, flat, scale_one, attn_gain_f)
    grad_input = dhidden + dh_one

    spread = lambda v: jnp.pad(
        v.reshape(shards, own_kv), ((0, 0), (0, own - own_kv))
    ).reshape(width)
    small_g = jnp.stack(
        [
            grad_bias[:width],
            grad_attn_gain,
            grad_mlp_gain,
            spread(grad_bias[width : width + kvd]),
            spread(grad_bias[width + kvd :]),
        ],
        axis=0,
    )
    small_g = jnp.pad(small_g, ((0, small_w - small_g.shape[0]), (0, 0))).T.astype(bf16)
    packed_g = jnp.concatenate([grad_qkv, grad_output, small_g], axis=1)
    owned = lax.psum_scatter(packed_g, "shard", scatter_dimension=0, tiled=True)
    total_w = wide + width
    share_w = total_w // reps
    chunks = [
        jnp.concatenate([owned[:, i * share_w : (i + 1) * share_w], owned[:, total_w:]], axis=1)
        for i in range(reps)
    ]
    split = lax.psum_scatter(
        jnp.concatenate(chunks, axis=0), "rep", scatter_dimension=0, tiled=True
    )
    vec = split[:, share_w : share_w + 5].astype(f32).T

    attn_all = lax.all_gather(split[:, :share_w], "rep", axis=0)
    attn_all = jnp.concatenate([attn_all[i] for i in range(reps)], axis=1).astype(f32)
    down_all = lax.all_gather(down_owned, "rep", axis=0, tiled=True).astype(f32)

    def joined(share):
        every = lax.all_gather(share, "rep", axis=0)
        return jnp.concatenate(
            [
                every[r][:, s * part : (s + 1) * part]
                for s in range(shards)
                for r in range(reps)
            ],
            axis=1,
        ).astype(f32)

    return (
        result,
        grad_input,
        attn_all[:, :width],
        attn_all[:, width : width + kvd],
        attn_all[:, width + kvd : wide],
        attn_all[:, wide:],
        vec[0],
        vec[3][:own_kv],
        vec[4][:own_kv],
        vec[1],
        joined(gate_owned),
        joined(up_owned),
        down_all,
        vec[2],
    )


def solution(mesh):
    in_specs = (
        P(("rep", "shard"), None),
        P(("rep", "shard"), None),
        P(("rep", "shard"), None),
        P("shard", None),
        P("shard", None),
        P("shard", None),
        P("shard", None),
        P("shard"),
        P("shard"),
        P("shard"),
        P("shard"),
        P("shard", None),
        P("shard", None),
        P("shard", None),
        P("shard"),
    )
    out_specs = (
        P(("rep", "shard"), None),
        P(("rep", "shard"), None),
        P("shard", None),
        P("shard", None),
        P("shard", None),
        P("shard", None),
        P("shard"),
        P("shard"),
        P("shard"),
        P("shard"),
        P("shard", None),
        P("shard", None),
        P("shard", None),
        P("shard"),
    )
    return jax.shard_map(
        on_device, mesh=mesh, in_specs=in_specs, out_specs=out_specs, check_vma=False
    )
```

```python
import math

import jax
import jax.numpy as jnp
from jax import lax
from jax.sharding import PartitionSpec as P

HEADS = 14
KVH = 2
HD = 64


theta_base = 1000000.0
eps_norm = 1e-06
masked_score = -1000000000.0


def times_transposed(left, weight):
    return lax.dot_general(
        left, weight, (((1,), (1,)), ((), ())), preferred_element_type=jnp.float32
    )


def tables(lengths_row, rows):
    ends = jnp.cumsum(lengths_row)
    starts = ends - lengths_row
    places = jnp.arange(rows, dtype=jnp.int32)
    inside = ((places[:, None] >= starts[None, :]) & (places[:, None] < ends[None, :])).astype(
        jnp.int32
    )
    slots = jnp.arange(lengths_row.shape[0], dtype=jnp.int32)
    segment = jnp.sum(inside * slots[None, :], axis=1)
    first = jnp.sum(inside * starts[None, :], axis=1)
    offset = (places - first).astype(jnp.float32)
    half = HD // 2
    freq = theta_base ** (-(jnp.arange(half, dtype=jnp.float32) * (2.0 / HD)))
    angles = offset[:, None] * freq[None, :]
    return (segment, places, jnp.cos(angles), jnp.sin(angles))


def rotate(values, cosine, sine):
    half = values.shape[-1] // 2
    first, second = (values[..., :half], values[..., half:])
    cosine = cosine[:, :, None, :]
    sine = sine[:, :, None, :]
    return jnp.concatenate(
        [first * cosine - second * sine, second * cosine + first * sine], axis=-1
    )


def unrotate(grads, cosine, sine):
    half = grads.shape[-1] // 2
    first, second = (grads[..., :half], grads[..., half:])
    cosine = cosine[:, :, None, :]
    sine = sine[:, :, None, :]
    return jnp.concatenate(
        [first * cosine + second * sine, second * cosine - first * sine], axis=-1
    )


def norm_fwd(hidden, gain):
    scale = lax.rsqrt(jnp.mean(hidden * hidden, axis=-1, keepdims=True) + eps_norm)
    return (scale, hidden * scale * gain.astype(jnp.float32))


def norm_bwd(dnormed, hidden, scale, gain):
    gain_f = gain.astype(jnp.float32)
    dgain = jnp.sum(dnormed * hidden * scale, axis=0)
    inner = dnormed * gain_f
    dhidden = scale * inner - hidden * (scale * scale * scale) * jnp.mean(
        inner * hidden, axis=-1, keepdims=True
    )
    return (dhidden, dgain)


def scores_of(query, keys, segment, places):
    raw = jnp.einsum("igha,jga->ghij", query, keys, preferred_element_type=jnp.float32) * (
        1.0 / math.sqrt(HD)
    )
    allowed = (segment[:, None] == segment[None, :]) & (places[None, :] <= places[:, None])
    return jnp.where(allowed[None, None], raw, masked_score)


def attend(query, keys, values, segment, places):
    raw = scores_of(query, keys, segment, places)
    top = jnp.max(raw, axis=-1, keepdims=True)
    total = jnp.sum(jnp.exp(raw - top), axis=-1)
    lse = top[..., 0] + jnp.log(total)
    probs = jnp.exp(raw - lse[..., None]).astype(jnp.bfloat16)
    mixed = jnp.einsum("ghij,jga->igha", probs, values, preferred_element_type=jnp.float32).astype(
        jnp.bfloat16
    )
    return (mixed, lse)


def attend_back(query, keys, values, mixed, dmixed, lse, segment, places):
    raw = scores_of(query, keys, segment, places)
    probs_f = jnp.exp(raw - lse[..., None])
    probs = probs_f.astype(jnp.bfloat16)
    dvals = jnp.einsum("ghij,igha->jga", probs, dmixed, preferred_element_type=jnp.float32)
    dprobs = jnp.einsum("igha,jga->ghij", dmixed, values, preferred_element_type=jnp.float32)
    delta = jnp.einsum("igha,igha->ghi", dmixed, mixed, preferred_element_type=jnp.float32)
    dscores = (probs_f * (dprobs - delta[..., None]) * (1.0 / math.sqrt(HD))).astype(jnp.bfloat16)
    dquery = jnp.einsum("ghij,jga->igha", dscores, keys, preferred_element_type=jnp.float32)
    dkeys = jnp.einsum("ghij,igha->jga", dscores, query, preferred_element_type=jnp.float32)
    return (dquery, dkeys, dvals)


def pad_rows(vector, rows):
    return jnp.pad(vector, (0, rows - vector.shape[0]))


def share_of(weight, index, shards, shares):
    width = weight.shape[1] // shards
    part = width // shares
    return jnp.concatenate(
        [
            lax.dynamic_slice(weight, (0, s * width + index * part), (weight.shape[0], part))
            for s in range(shards)
        ],
        axis=1,
    )


def row_pieces(array, count):
    rows = array.shape[0]
    step = -(-rows // count)
    step = min(rows, -(-step // 8) * 8)
    return [array[i : min(i + step, rows)] for i in range(0, rows, step)]


def fold(blocks, wide):
    count, rows, cols = blocks.shape
    if rows % 8 or cols % 128 or (rows // 8) * 128 != wide:
        return blocks.reshape(count, rows * cols // wide, wide)
    tiles = blocks.reshape(count, rows // 8, 8, cols // 128, 128)
    return tiles.transpose(0, 3, 2, 1, 4).reshape(count, cols // 16, wide)


def unfold(blocks, rows, cols):
    count, _, wide = blocks.shape
    if rows % 8 or cols % 128 or (rows // 8) * 128 != wide:
        return blocks.reshape(count, rows, cols)
    tiles = blocks.reshape(count, cols // 128, 8, rows // 8, 128)
    return tiles.transpose(0, 3, 2, 1, 4).reshape(count, rows, cols)


def on_device(
    tokens,
    cotangent,
    lengths,
    query_weight,
    key_weight,
    value_weight,
    output_weight,
    query_bias,
    key_bias,
    value_bias,
    attn_gain,
    gate_weight,
    up_weight,
    down_weight,
    mlp_gain,
):
    shards = lax.axis_size("shard")
    reps = lax.axis_size("rep")
    rep = lax.axis_index("rep")
    rows, width = tokens.shape
    own = query_weight.shape[0]
    kvd = key_weight.shape[1]
    own_kv = key_bias.shape[0]
    small_w = 128
    f32, bf16 = jnp.float32, jnp.bfloat16

    small = jnp.stack(
        [query_bias, attn_gain, mlp_gain, pad_rows(key_bias, own), pad_rows(value_bias, own)],
        axis=1,
    )
    small = jnp.pad(small, ((0, 0), (0, small_w - small.shape[1])))
    packed = jnp.concatenate(
        [query_weight, key_weight, value_weight, output_weight, small], axis=1
    )
    packed = lax.all_gather(packed, "shard", axis=0, tiled=True)
    wide = width + 2 * kvd
    qkv_weight = packed[:, :wide]
    output_full = packed[:, wide : wide + width]
    vectors = packed[:, wide + width : wide + width + 5].T
    query_bias_f, attn_gain_f, mlp_gain_f = vectors[0], vectors[1], vectors[2]
    key_bias_f = vectors[3].reshape(shards, own)[:, :own_kv].reshape(kvd)
    value_bias_f = vectors[4].reshape(shards, own)[:, :own_kv].reshape(kvd)
    qkv_bias = jnp.concatenate([query_bias_f, key_bias_f, value_bias_f]).astype(f32)

    part = down_weight.shape[0] // reps
    both_mine = lax.all_gather(
        jnp.concatenate(
            [share_of(gate_weight, rep, shards, reps), share_of(up_weight, rep, shards, reps)],
            axis=1,
        ),
        "shard",
        axis=0,
        tiled=True,
    )
    down_part = lax.dynamic_slice(down_weight, (rep * part, 0), (part, width))
    down_mine = jnp.concatenate(
        [lax.all_gather(p, "shard", axis=0) for p in row_pieces(down_part, 3)], axis=1
    ).reshape(shards * part, width)
    cot_all = lax.all_gather(cotangent, "rep", axis=0, tiled=True)

    segment, places, cosine, sine = jax.vmap(lambda lens: tables(lens, rows))(lengths)
    flat = tokens.astype(f32)
    scale_one, normed_one = norm_fwd(flat, attn_gain_f)
    normed_one = normed_one.astype(bf16)
    qkv = jnp.dot(normed_one, qkv_weight, preferred_element_type=f32) + qkv_bias
    query = rotate(qkv[:, :width].reshape(1, rows, HEADS, HD), cosine, sine).astype(bf16)
    query = query.reshape(1, rows, KVH, HEADS // KVH, HD)
    keys = rotate(qkv[:, width : width + kvd].reshape(1, rows, KVH, HD), cosine, sine).astype(bf16)
    values = qkv[:, width + kvd :].reshape(1, rows, KVH, HD).astype(bf16)
    mixed, lse = jax.vmap(attend)(query, keys, values, segment, places)
    mixed_flat = mixed.reshape(rows, width)
    hidden_one = flat + jnp.dot(mixed_flat, output_full, preferred_element_type=f32)
    scale_two, normed_two = norm_fwd(hidden_one, mlp_gain_f)
    normed_all = lax.all_gather(normed_two.astype(bf16), "rep", axis=0, tiled=True)

    both = jnp.dot(normed_all, both_mine, preferred_element_type=f32)
    hidden = both.shape[1] // 2
    gate, upper = both[:, :hidden], both[:, hidden:]
    sigma = jax.nn.sigmoid(gate)
    product = (gate * sigma * upper).astype(bf16)
    dprod = times_transposed(cot_all, down_mine)
    dgate = (dprod * upper * sigma * (1.0 + gate * (1.0 - sigma))).astype(bf16)
    dup = (dprod * gate * sigma).astype(bf16)
    dboth = jnp.concatenate([dgate, dup], axis=1)
    dnormed_part = times_transposed(dboth, both_mine).astype(bf16)
    out_part = jnp.dot(product, down_mine, preferred_element_type=f32).astype(bf16)
    sums = lax.psum_scatter(
        jnp.concatenate([dnormed_part, out_part], axis=1), "rep", scatter_dimension=0, tiled=True
    ).astype(f32)
    dnormed_two, out_sum = sums[:, :width], sums[:, width:]
    result = (hidden_one + out_sum).astype(bf16)
    grad_down = jnp.dot(product.T, cot_all, preferred_element_type=f32).astype(bf16)
    grad_both = jnp.dot(normed_all.T, dboth, preferred_element_type=f32).astype(bf16)
    mlp_owned = lax.psum_scatter(
        jnp.concatenate(
            [
                grad_both.reshape(shards, own, 2 * hidden),
                fold(grad_down.reshape(shards, part, width), 2 * hidden),
            ],
            axis=1,
        ).reshape(-1, 2 * hidden),
        "shard",
        scatter_dimension=0,
        tiled=True,
    )
    mlp_owned = lax.optimization_barrier(mlp_owned)

    dh_two, grad_mlp_gain = norm_bwd(dnormed_two, hidden_one, scale_two, mlp_gain_f)
    dhidden = cotangent.astype(f32) + dh_two
    dres = dhidden.astype(bf16)
    grad_output = jnp.dot(mixed_flat.T, dres, preferred_element_type=f32).astype(bf16)
    dmixed = times_transposed(dres, output_full).astype(bf16)
    dmixed = dmixed.reshape(1, rows, KVH, HEADS // KVH, HD)
    dquery, dkeys, dvals = jax.vmap(attend_back)(
        query, keys, values, mixed, dmixed, lse, segment, places
    )
    dquery = unrotate(dquery.reshape(1, rows, HEADS, HD), cosine, sine).reshape(rows, width)
    dkeys = unrotate(dkeys, cosine, sine).reshape(rows, kvd)
    dvals = dvals.reshape(rows, kvd)
    dqkv = jnp.concatenate([dquery, dkeys, dvals], axis=1)
    grad_bias = jnp.sum(dqkv, axis=0)
    dqkv_b = dqkv.astype(bf16)
    grad_qkv = jnp.dot(normed_one.T, dqkv_b, preferred_element_type=f32).astype(bf16)
    dnormed_one = times_transposed(dqkv_b, qkv_weight)
    dh_one, grad_attn_gain = norm_bwd(dnormed_one, flat, scale_one, attn_gain_f)
    grad_input = dhidden + dh_one

    spread = lambda v: jnp.pad(
        v.reshape(shards, own_kv), ((0, 0), (0, own - own_kv))
    ).reshape(width)
    small_g = jnp.stack(
        [
            grad_bias[:width],
            grad_attn_gain,
            grad_mlp_gain,
            spread(grad_bias[width : width + kvd]),
            spread(grad_bias[width + kvd :]),
        ],
        axis=0,
    )
    small_g = jnp.pad(small_g, ((0, small_w - small_g.shape[0]), (0, 0))).T.astype(bf16)
    packed_g = jnp.concatenate([grad_qkv, grad_output, small_g], axis=1)
    owned = lax.psum_scatter(packed_g, "shard", scatter_dimension=0, tiled=True)
    total_w = wide + width
    share_w = total_w // reps
    chunks = [
        jnp.concatenate([owned[:, i * share_w : (i + 1) * share_w], owned[:, total_w:]], axis=1)
        for i in range(reps)
    ]
    split = lax.psum_scatter(
        jnp.concatenate(chunks, axis=0), "rep", scatter_dimension=0, tiled=True
    )
    vec = split[:, share_w : share_w + 5].astype(f32).T

    attn_all = lax.all_gather(split[:, :share_w], "rep", axis=0)
    attn_all = jnp.concatenate([attn_all[i] for i in range(reps)], axis=1).astype(f32)

    def from_replicas(share):
        limit = max(1, (240 * 1024) // (2 * share.shape[1]))
        count = -(-share.shape[0] // limit)
        return jnp.concatenate(
            [lax.all_gather(p, "rep", axis=0) for p in row_pieces(share, count)], axis=1
        )

    both_all = from_replicas(mlp_owned[:own])
    down_all = unfold(from_replicas(mlp_owned[own:]), part, width)
    down_all = down_all.reshape(reps * part, width).astype(f32)

    def joined(first):
        return jnp.concatenate(
            [
                both_all[r][:, first + s * part : first + (s + 1) * part]
                for s in range(shards)
                for r in range(reps)
            ],
            axis=1,
        ).astype(f32)

    return (
        result,
        grad_input,
        attn_all[:, :width],
        attn_all[:, width : width + kvd],
        attn_all[:, width + kvd : wide],
        attn_all[:, wide:],
        vec[0],
        vec[3][:own_kv],
        vec[4][:own_kv],
        vec[1],
        joined(0),
        joined(hidden),
        down_all,
        vec[2],
    )


def solution(mesh):
    in_specs = (
        P(("rep", "shard"), None),
        P(("rep", "shard"), None),
        P(("rep", "shard"), None),
        P("shard", None),
        P("shard", None),
        P("shard", None),
        P("shard", None),
        P("shard"),
        P("shard"),
        P("shard"),
        P("shard"),
        P("shard", None),
        P("shard", None),
        P("shard", None),
        P("shard"),
    )
    out_specs = (
        P(("rep", "shard"), None),
        P(("rep", "shard"), None),
        P("shard", None),
        P("shard", None),
        P("shard", None),
        P("shard", None),
        P("shard"),
        P("shard"),
        P("shard"),
        P("shard"),
        P("shard", None),
        P("shard", None),
        P("shard", None),
        P("shard"),
    )
    return jax.shard_map(
        on_device, mesh=mesh, in_specs=in_specs, out_specs=out_specs, check_vma=False
    )
```
